32 devices in a mesh: groups: 2 (over y), seq: 4 (over z), rows: 4 (over x, core).
Axes of the slice: x: 2, y: 2, z: 4, core: 2. Of those that a mesh axis runs over, the one named last changes fastest.
Arguments:
- layer_inputs: bfloat16 [8, 128, 4096], P(('groups', 'rows'), 'seq'), parts along dimension 0, may hold values from -6 to 6
- out_grads: bfloat16 [8, 128, 4096], P(('groups', 'rows'), 'seq'), parts along dimension 0, may hold values from -6 to 6
- input_proj: bfloat16 [4096, 128], P('seq'), may hold values from -0.09375 to 0.09375
- grad_proj: bfloat16 [4096, 128], P('seq'), may hold values from -0.09375 to 0.09375
- query_lengths: int32 [8], P(('groups', 'rows')), parts along dimension 0, may hold values from 1 to 128, as said below
- train_store: float32 [2048, 16384], P(('groups', 'rows'), 'seq'), parts along dimension 0, may hold values from -0.00390625 to 0.00390625
Outputs:
- influence: float32 [8, 1024], P(('groups', 'seq'), 'rows'), parts along dimension 0
The draws below stay inside these ranges and needn't reach their ends.
There are 2 independent parts, one for each index of `groups`. The reference program is written for one: setup_inputs(seed, part) draws one part's arguments, and reference() takes and returns one part's arrays. A program takes and returns all parts, laid end to end along the dimension named above; an argument that names none is the same for every part. Nothing has to cross between parts.
Inputs may be any that keep to these rules, and one draw needn't show every extreme that they name: `query_lengths`: some query of every draw has all 128 tokens.
All inputs are finite; a program needn't handle non-finite values.
Results may differ from the reference program's by a relative error of at most 0.0003.
Values may be sent and summed in bfloat16 or wider, within the bound.
No kernel may reach another device: no remote copies, remote signals or barrier semaphores. Data moves between devices by JAX's collectives and lax.ppermute only.
A program may use at most 64 MiB of HBM per device.

```python
import jax
import jax.numpy as jnp
from jax import lax

D = 4096
K = 128
Q = 4
L = 128
R = 1024
C = 16384


def draw_query_lengths(key, part):
    values = jax.random.randint(jax.random.fold_in(key, 11), (Q,), 1, L + 1)
    chosen = jax.random.randint(jax.random.fold_in(key, 12), (), 0, Q)
    return jnp.where(jnp.arange(Q) == chosen, L, values).astype(jnp.int32)


def levels(stream_key, extent, shards, least, high):
    level, own = 1.0, jax.random.fold_in(stream_key, 6)
    for position, blocks in shards:
        draws = jnp.exp(jax.random.uniform(jax.random.fold_in(own, position), (blocks,), jnp.float32, least / len(shards), high / len(shards)))
        level = level * jnp.repeat(draws, extent[position] // blocks).reshape([-1 if axis == position else 1 for axis in range(len(extent))])
    return level


def gaussian(key, shape, spread, bound, shards=(), kind=jnp.bfloat16):
    values = spread * jax.random.normal(key, shape, jnp.float32)
    if shards:
        values = values * levels(key, shape, shards, -0.22, 0.18)
    return jnp.clip(values, -bound, bound).astype(kind)


def setup_inputs(seed: int = 0, part: int = 0) -> dict:
    splits = jax.random.split(jax.random.key(seed), 7)
    own_keys = jax.random.split(jax.random.fold_in(splits[6], part), 7)
    return {
        "layer_inputs": gaussian(own_keys[0], (Q, L, D), 1.0, 6.0, ((0, 4), (1, 4))),
        "out_grads": gaussian(own_keys[1], (Q, L, D), 1.0, 6.0, ((0, 4), (1, 4))),
        "input_proj": gaussian(splits[2], (D, K), D ** -0.5, 0.09375, ((0, 4),)),
        "grad_proj": gaussian(splits[3], (D, K), D ** -0.5, 0.09375, ((0, 4),)),
        "query_lengths": draw_query_lengths(jax.random.fold_in(jax.random.fold_in(splits[6], part), 71), part),
        "train_store": gaussian(own_keys[5], (R, C), (C * L) ** -0.5, 0.00390625, ((0, 4), (1, 4)), jnp.float32),
    }


def reference(layer_inputs, out_grads, input_proj, grad_proj, query_lengths, train_store):
    n_query, n_tok, width = layer_inputs.shape
    feat_in = jnp.dot(layer_inputs.reshape(n_query * n_tok, width), input_proj, preferred_element_type=jnp.float32).reshape(n_query, n_tok, -1)
    feat_out = jnp.dot(out_grads.reshape(n_query * n_tok, width), grad_proj, preferred_element_type=jnp.float32).reshape(n_query, n_tok, -1)
    positions = jnp.arange(n_tok, dtype=jnp.int32)
    validity = (positions[None, :] < query_lengths[:, None]).astype(jnp.float32)
    feat_out = feat_out * validity[:, :, None]
    query_grad = jnp.einsum("qti,qtj->qij", feat_out, feat_in, precision=lax.Precision.HIGHEST).reshape(n_query, -1)
    return lax.dot_general(query_grad, train_store, (((1,), (1,)), ((), ())), precision=lax.Precision.HIGHEST, preferred_element_type=jnp.float32)
```

```python
import functools

import jax
import jax.numpy as jnp
from jax import lax
from jax.experimental import pallas as pl
from jax.experimental.pallas import tpu as pltpu
from jax.sharding import PartitionSpec as P


LANES = 128
VMEM = pl.BlockSpec(memory_space=pltpu.VMEM)
HBM = pl.BlockSpec(memory_space=pl.ANY)
SMEM = pl.BlockSpec(memory_space=pltpu.SMEM)


def partners(n):
    if n & (n - 1) == 0:
        return (lambda d, k: d ^ k), (lambda d, k: d ^ k)
    return (lambda d, k: (d + k) % n), (lambda d, k: (d - k + n) % n)


def exchange(arrays, axis, n):
    to, _ = partners(n)
    return [
        lax.ppermute(arrays[k - 1], axis, [(d, to(d, k)) for d in range(n)])
        for k in range(1, n)
    ]


def call(kernel, outs, in_specs, scratch=(), mib=16):
    return pl.pallas_call(
        kernel,
        out_shape=[jax.ShapeDtypeStruct(*o) for o in outs],
        in_specs=list(in_specs),
        out_specs=[VMEM] * len(outs),
        scratch_shapes=list(scratch),
        compiler_params=pltpu.CompilerParams(vmem_limit_bytes=mib << 20),
    )


def pack_kernel(x, g, *rest, n, width):
    outs, sem = rest[:n], rest[n]
    to, _ = partners(n)
    s = lax.axis_index("seq")
    copies = []
    for k in list(range(1, n)) + [0]:
        at = pl.multiple_of(to(s, k) * width, width)
        for j, src in enumerate((x, g)):
            copies.append(
                pltpu.make_async_copy(src.at[0, :, pl.ds(at, width)], outs[k].at[j], sem.at[k, j])
            )
    for c in copies:
        c.start()
    for c in copies:
        c.wait()


def feature_kernel(*refs, n, n_tok, block):
    toks, w_in, w_out = refs[:n], refs[n], refs[n + 1]
    outs, rows = refs[n + 2 : 2 * n + 2], refs[2 * n + 2]
    to, source = partners(n)
    s = lax.axis_index("seq")
    total = n * n_tok
    for k in range(n):
        at = pl.multiple_of(source(s, k) * n_tok, n_tok)
        for j in range(2):
            rows[j, pl.ds(at, n_tok), :] = toks[k][j]
    first = jnp.dot(rows[0], w_in[...], preferred_element_type=jnp.float32)
    second = jnp.dot(rows[1], w_out[...], preferred_element_type=jnp.float32)
    turned = refs[2 * n + 3]
    for c in range(total // LANES):
        turned[c] = second[c * LANES : (c + 1) * LANES].T
    for k in range(n):
        at = pl.multiple_of(to(s, k) * block, block)
        outs[k][:total] = first
        for c in range(total // LANES):
            outs[k][total + c * block : total + (c + 1) * block] = turned[c, pl.ds(at, block), :]


def gradient_kernel(length, *refs, n, total, block):
    parts, out = refs[:n], refs[n]
    whole = parts[0][...]
    for part in parts[1:]:
        whole = whole + part[...]
    acc = None
    for c in range(total // LANES):
        feat_out = whole[total + c * block : total + (c + 1) * block]
        at = c * LANES + lax.broadcasted_iota(jnp.int32, feat_out.shape, 1)
        feat_out = jnp.where(at < length[0], feat_out, 0.0)
        prod = jnp.dot(
            feat_out,
            whole[c * LANES : (c + 1) * LANES],
            precision=lax.Precision.HIGHEST,
            preferred_element_type=jnp.float32,
        )
        acc = prod if acc is None else acc + prod
    out[...] = acc


def score_kernel(*refs, n, m, block, n_rows, step):
    grads, store = refs[:m], refs[m]
    outs, scores = refs[m + 1 : m + 1 + n], refs[m + 1 + n]
    to, _ = partners(n)
    s, r = lax.axis_index("seq"), lax.axis_index("rows")

    def rows_step(t, carry):
        at = pl.multiple_of(t * step, step)
        acc = [jnp.zeros((step, LANES), jnp.float32) for _ in range(m)]
        for i in range(block):
            tile = store[pl.ds(at, step), i * LANES : (i + 1) * LANES]
            for k in range(m):
                acc[k] = acc[k] + tile * grads[k][i : i + 1, :]
        for k in range(m):
            scores[k, pl.ds(at, step), :] = acc[k]
        return carry

    lax.fori_loop(0, n_rows // step, rows_step, 0)
    for k in range(n):
        q = to(s, k)
        mine = r ^ q
        outs[k][...] = jnp.sum(scores[mine], axis=1)[None, :]


def body(layer_inputs, out_grads, input_proj, grad_proj, query_lengths, train_store):
    n, m = lax.axis_size("seq"), lax.axis_size("rows")
    n_query, n_tok, width = layer_inputs.shape
    total = n * n_tok
    part, feats = input_proj.shape
    n_rows, coords = train_store.shape
    block = coords // feats
    f32 = jnp.float32

    packed = call(
        functools.partial(pack_kernel, n=n, width=part),
        [((2, n_tok, part), layer_inputs.dtype)] * n,
        [HBM, HBM],
        [pltpu.SemaphoreType.DMA((n, 2))],
    )(layer_inputs, out_grads)
    tokens = [packed[0]] + exchange(packed[1:], "seq", n)

    height = total + total * block // LANES
    partial = call(
        functools.partial(feature_kernel, n=n, n_tok=n_tok, block=block),
        [((height, LANES), f32)] * n,
        [VMEM] * (n + 2),
        [pltpu.VMEM((2, total, part), layer_inputs.dtype), pltpu.VMEM((total // LANES, feats, LANES), f32)],
    )(*tokens, input_proj, grad_proj)
    parts = [partial[0]] + exchange(partial[1:], "seq", n)

    (grad,) = call(
        functools.partial(gradient_kernel, n=n, total=total, block=block),
        [((block, LANES), f32)],
        [SMEM] + [VMEM] * n,
    )(query_lengths, *parts)
    grads = [grad] + exchange([grad] * (m - 1), "rows", m)

    scores = call(
        functools.partial(score_kernel, n=n, m=m, block=block, n_rows=n_rows, step=64 if m <= 4 else 8),
        [((1, n_rows), f32)] * n,
        [VMEM] * (m + 1),
        [pltpu.VMEM((m, n_rows, LANES), f32)],
    )(*grads, train_store)
    out = scores[0]
    for other in exchange(scores[1:], "seq", n):
        out = out + other
    return out


def solution(mesh):
    in_specs = (
        P(("groups", "rows"), "seq", None),
        P(("groups", "rows"), "seq", None),
        P("seq", None),
        P("seq", None),
        P(("groups", "rows")),
        P(("groups", "rows"), "seq"),
    )
    out_specs = P(("groups", "seq"), "rows")
    return jax.shard_map(body, mesh=mesh, in_specs=in_specs, out_specs=out_specs, check_vma=False)
```

```python
import functools

import jax
import jax.numpy as jnp
from jax import lax
from jax.experimental import pallas as pl
from jax.experimental.pallas import tpu as pltpu
from jax.sharding import PartitionSpec as P


LANES = 128
VMEM = pl.BlockSpec(memory_space=pltpu.VMEM)
HBM = pl.BlockSpec(memory_space=pltpu.HBM)
SMEM = pl.BlockSpec(memory_space=pltpu.SMEM)


def partners(n):
    if n & (n - 1) == 0:
        return (lambda d, k: d ^ k), (lambda d, k: d ^ k)
    return (lambda d, k: (d + k) % n), (lambda d, k: (d - k + n) % n)


def exchange(arrays, axis, n):
    to, _ = partners(n)
    return [
        lax.ppermute(arrays[k - 1], axis, [(d, to(d, k)) for d in range(n)])
        for k in range(1, n)
    ]


def in_place(array):
    return pltpu.with_memory_space_constraint(array, pltpu.HBM)


def call(kernel, outs, in_specs, scratch=(), mib=16):
    return pl.pallas_call(
        kernel,
        out_shape=[jax.ShapeDtypeStruct(*o) for o in outs],
        in_specs=list(in_specs),
        out_specs=[VMEM] * len(outs),
        scratch_shapes=list(scratch),
        compiler_params=pltpu.CompilerParams(vmem_limit_bytes=mib << 20),
    )


def pack_kernel(x, g, *rest, n, width):
    outs, sem = rest[:n], rest[n]
    to, _ = partners(n)
    s = lax.axis_index("seq")
    copies = []
    for k in list(range(1, n)) + [0]:
        at = pl.multiple_of(to(s, k) * width, width)
        for j, src in enumerate((x, g)):
            copies.append(
                pltpu.make_async_copy(src.at[0, :, pl.ds(at, width)], outs[k].at[j], sem.at[k, j])
            )
    for c in copies:
        c.start()
    for c in copies:
        c.wait()


def fetch_kernel(*refs):
    count = (len(refs) - 2) // 2
    sources, outs, sem = refs[1 : count + 1], refs[count + 1 : -1], refs[-1]
    copies = [
        pltpu.make_async_copy(src, out, sem.at[j]) for j, (src, out) in enumerate(zip(sources, outs))
    ]
    for c in copies:
        c.start()
    for c in copies:
        c.wait()


def feature_kernel(*refs, n, n_tok, block):
    toks, w_in, w_out = refs[:n], refs[n], refs[n + 1]
    outs, rows = refs[n + 2 : 2 * n + 2], refs[2 * n + 2]
    to, source = partners(n)
    s = lax.axis_index("seq")
    total = n * n_tok
    for k in range(n):
        at = pl.multiple_of(source(s, k) * n_tok, n_tok)
        for j in range(2):
            rows[j, pl.ds(at, n_tok), :] = toks[k][j]
    first = jnp.dot(rows[0], w_in[...], preferred_element_type=jnp.float32)
    second = jnp.dot(rows[1], w_out[...], preferred_element_type=jnp.float32)
    turned = refs[2 * n + 3]
    for c in range(total // LANES):
        turned[c] = second[c * LANES : (c + 1) * LANES].T
    for k in range(n):
        at = pl.multiple_of(to(s, k) * block, block)
        outs[k][:total] = first
        for c in range(total // LANES):
            outs[k][total + c * block : total + (c + 1) * block] = turned[c, pl.ds(at, block), :]


def gradient_kernel(length, *refs, n, total, block):
    parts, out = refs[:n], refs[n]
    whole = parts[0][...]
    for part in parts[1:]:
        whole = whole + part[...]
    acc = None
    for c in range(total // LANES):
        feat_out = whole[total + c * block : total + (c + 1) * block]
        at = c * LANES + lax.broadcasted_iota(jnp.int32, feat_out.shape, 1)
        feat_out = jnp.where(at < length[0], feat_out, 0.0)
        prod = jnp.dot(
            feat_out,
            whole[c * LANES : (c + 1) * LANES],
            precision=lax.Precision.HIGHEST,
            preferred_element_type=jnp.float32,
        )
        acc = prod if acc is None else acc + prod
    out[...] = acc


def score_kernel(*refs, n, m, block, n_rows, step):
    grads, store = refs[:m], refs[m]
    outs, scores = refs[m + 1 : m + 1 + n], refs[m + 1 + n]
    to, _ = partners(n)
    s, r = lax.axis_index("seq"), lax.axis_index("rows")

    def rows_step(t, carry):
        at = pl.multiple_of(t * step, step)
        acc = [jnp.zeros((step, LANES), jnp.float32) for _ in range(m)]
        for i in range(block):
            tile = store[pl.ds(at, step), i * LANES : (i + 1) * LANES]
            for k in range(m):
                acc[k] = acc[k] + tile * grads[k][i : i + 1, :]
        for k in range(m):
            scores[k, pl.ds(at, step), :] = acc[k]
        return carry

    lax.fori_loop(0, n_rows // step, rows_step, 0)
    for k in range(n):
        q = to(s, k)
        mine = r ^ q
        outs[k][...] = jnp.sum(scores[mine], axis=1)[None, :]


def body(layer_inputs, out_grads, input_proj, grad_proj, query_lengths, train_store):
    n, m = lax.axis_size("seq"), lax.axis_size("rows")
    n_query, n_tok, width = layer_inputs.shape
    total = n * n_tok
    part, feats = input_proj.shape
    n_rows, coords = train_store.shape
    block = coords // feats
    f32 = jnp.float32

    packed = call(
        functools.partial(pack_kernel, n=n, width=part),
        [((2, n_tok, part), layer_inputs.dtype)] * n,
        [HBM, HBM],
        [pltpu.SemaphoreType.DMA((n, 2))],
    )(in_place(layer_inputs), in_place(out_grads))
    held = (input_proj, grad_proj, train_store)
    input_proj, grad_proj, train_store = call(
        fetch_kernel,
        [(a.shape, a.dtype) for a in held],
        [VMEM] + [HBM] * 3,
        [pltpu.SemaphoreType.DMA((3,))],
    )(packed[0], *map(in_place, held))
    tokens = [packed[0]] + exchange(packed[1:], "seq", n)

    height = total + total * block // LANES
    partial = call(
        functools.partial(feature_kernel, n=n, n_tok=n_tok, block=block),
        [((height, LANES), f32)] * n,
        [VMEM] * (n + 2),
        [pltpu.VMEM((2, total, part), layer_inputs.dtype), pltpu.VMEM((total // LANES, feats, LANES), f32)],
    )(*tokens, input_proj, grad_proj)
    parts = [partial[0]] + exchange(partial[1:], "seq", n)

    (grad,) = call(
        functools.partial(gradient_kernel, n=n, total=total, block=block),
        [((block, LANES), f32)],
        [SMEM] + [VMEM] * n,
    )(query_lengths, *parts)
    grads = [grad] + exchange([grad] * (m - 1), "rows", m)

    scores = call(
        functools.partial(score_kernel, n=n, m=m, block=block, n_rows=n_rows, step=64 if m <= 4 else 8),
        [((1, n_rows), f32)] * n,
        [VMEM] * (m + 1),
        [pltpu.VMEM((m, n_rows, LANES), f32)],
    )(*grads, train_store)
    out = scores[0]
    for other in exchange(scores[1:], "seq", n):
        out = out + other
    return out


def solution(mesh):
    in_specs = (
        P(("groups", "rows"), "seq", None),
        P(("groups", "rows"), "seq", None),
        P("seq", None),
        P("seq", None),
        P(("groups", "rows")),
        P(("groups", "rows"), "seq"),
    )
    out_specs = P(("groups", "seq"), "rows")
    return jax.shard_map(body, mesh=mesh, in_specs=in_specs, out_specs=out_specs, check_vma=False)
```

```python
import functools

import jax
import jax.numpy as jnp
from jax import lax
from jax.experimental import pallas as pl
from jax.experimental.pallas import tpu as pltpu
from jax.sharding import PartitionSpec as P


LANES = 128
VMEM = pl.BlockSpec(memory_space=pltpu.VMEM)
HBM = pl.BlockSpec(memory_space=pltpu.HBM)
SMEM = pl.BlockSpec(memory_space=pltpu.SMEM)


def partners(n):
    if n & (n - 1) == 0:
        return (lambda d, k: d ^ k), (lambda d, k: d ^ k)
    return (lambda d, k: (d + k) % n), (lambda d, k: (d - k + n) % n)


def exchange(arrays, axis, n):
    to, _ = partners(n)
    got = []
    for k in range(1, n):
        got.append(lax.ppermute(arrays[k - 1], axis, [(d, to(d, k)) for d in range(n)]))
    return got


def in_place(array):
    return pltpu.with_memory_space_constraint(array, pltpu.HBM)


def call(kernel, outs, in_specs, scratch=(), mib=16):
    return pl.pallas_call(
        kernel,
        out_shape=[jax.ShapeDtypeStruct(*o) for o in outs],
        in_specs=list(in_specs),
        out_specs=[VMEM] * len(outs),
        scratch_shapes=list(scratch),
        compiler_params=pltpu.CompilerParams(vmem_limit_bytes=mib << 20),
    )


def pack_kernel(x, g, *rest, n, width):
    outs, sem = rest[:n], rest[n]
    to, _ = partners(n)
    s = lax.axis_index("seq")
    copies = []
    for k in list(range(1, n)) + [0]:
        at = pl.multiple_of(to(s, k) * width, width)
        for j, src in enumerate((x, g)):
            copies.append(
                pltpu.make_async_copy(src.at[0, :, pl.ds(at, width)], outs[k].at[j], sem.at[k, j])
            )
    for c in copies:
        c.start()
    for c in copies:
        c.wait()


def fetch_kernel(*refs):
    count = (len(refs) - 2) // 2
    sources, outs, sem = refs[1 : count + 1], refs[count + 1 : -1], refs[-1]
    copies = [
        pltpu.make_async_copy(src, out, sem.at[j]) for j, (src, out) in enumerate(zip(sources, outs))
    ]
    for c in copies:
        c.start()
    for c in copies:
        c.wait()


def feature_kernel(*refs, n, n_tok, block):
    toks, w_in, w_out = refs[:n], refs[n], refs[n + 1]
    outs, rows = refs[n + 2 : 2 * n + 2], refs[2 * n + 2]
    to, source = partners(n)
    s = lax.axis_index("seq")
    total = n * n_tok
    for k in range(n):
        at = pl.multiple_of(source(s, k) * n_tok, n_tok)
        for j in range(2):
            rows[j, pl.ds(at, n_tok), :] = toks[k][j]
    first = jnp.dot(rows[0], w_in[...], preferred_element_type=jnp.float32)
    second = jnp.dot(rows[1], w_out[...], preferred_element_type=jnp.float32)
    turned = refs[2 * n + 3]
    for c in range(total // LANES):
        turned[c] = second[c * LANES : (c + 1) * LANES].T
    for k in range(n):
        at = pl.multiple_of(to(s, k) * block, block)
        outs[k][:total] = first
        for c in range(total // LANES):
            outs[k][total + c * block : total + (c + 1) * block] = turned[c, pl.ds(at, block), :]


def gradient_kernel(length, *refs, n, total, block):
    parts, out = refs[:n], refs[n]
    whole = parts[0][...]
    for part in parts[1:]:
        whole = whole + part[...]
    acc = None
    for c in range(total // LANES):
        feat_out = whole[total + c * block : total + (c + 1) * block]
        at = c * LANES + lax.broadcasted_iota(jnp.int32, feat_out.shape, 1)
        feat_out = jnp.where(at < length[0], feat_out, 0.0)
        prod = jnp.dot(
            feat_out,
            whole[c * LANES : (c + 1) * LANES],
            precision=lax.Precision.HIGHEST,
            preferred_element_type=jnp.float32,
        )
        acc = prod if acc is None else acc + prod
    out[...] = acc


def score_kernel(*refs, n, m, block, n_rows, step):
    grads, store = refs[:m], refs[m]
    outs, scores = refs[m + 1 : m + 1 + n], refs[m + 1 + n]
    to, _ = partners(n)
    s, r = lax.axis_index("seq"), lax.axis_index("rows")

    def rows_step(t, carry):
        at = pl.multiple_of(t * step, step)
        acc = [jnp.zeros((step, LANES), jnp.float32) for _ in range(m)]
        for i in range(block):
            tile = store[pl.ds(at, step), i * LANES : (i + 1) * LANES]
            for k in range(m):
                acc[k] = acc[k] + tile * grads[k][i : i + 1, :]
        for k in range(m):
            scores[k, pl.ds(at, step), :] = acc[k]
        return carry

    lax.fori_loop(0, n_rows // step, rows_step, 0)
    for k in range(n):
        q = to(s, k)
        mine = r ^ q
        outs[k][...] = jnp.sum(scores[mine], axis=1)[None, :]


def body(layer_inputs, out_grads, input_proj, grad_proj, query_lengths, train_store):
    n, m = lax.axis_size("seq"), lax.axis_size("rows")
    _, n_tok, _ = layer_inputs.shape
    total = n * n_tok
    part, feats = input_proj.shape
    n_rows, coords = train_store.shape
    block = coords // feats
    f32 = jnp.float32

    packed = call(
        functools.partial(pack_kernel, n=n, width=part),
        [((2, n_tok, part), layer_inputs.dtype)] * n,
        [HBM, HBM],
        [pltpu.SemaphoreType.DMA((n, 2))],
    )(in_place(layer_inputs), in_place(out_grads))
    held = (input_proj, grad_proj, train_store)
    input_proj, grad_proj, train_store = call(
        fetch_kernel,
        [(a.shape, a.dtype) for a in held],
        [VMEM] + [HBM] * 3,
        [pltpu.SemaphoreType.DMA((3,))],
    )(packed[0], *map(in_place, held))
    tokens = [packed[0]] + exchange(packed[1:], "seq", n)

    height = total + total * block // LANES
    partial = call(
        functools.partial(feature_kernel, n=n, n_tok=n_tok, block=block),
        [((height, LANES), f32)] * n,
        [VMEM] * (n + 2),
        [pltpu.VMEM((2, total, part), layer_inputs.dtype), pltpu.VMEM((total // LANES, feats, LANES), f32)],
    )(*tokens, input_proj, grad_proj)
    parts = [partial[0]] + exchange(partial[1:], "seq", n)

    (grad,) = call(
        functools.partial(gradient_kernel, n=n, total=total, block=block),
        [((block, LANES), f32)],
        [SMEM] + [VMEM] * n,
    )(query_lengths, *parts)
    grads = [grad] + exchange([grad] * (m - 1), "rows", m)

    scores = call(
        functools.partial(score_kernel, n=n, m=m, block=block, n_rows=n_rows, step=64 if m <= 4 else 8),
        [((1, n_rows), f32)] * n,
        [VMEM] * (m + 1),
        [pltpu.VMEM((m, n_rows, LANES), f32)],
    )(*grads, train_store)
    out = scores[0]
    for other in exchange(scores[1:], "seq", n):
        out = out + other
    return out


def solution(mesh):
    in_specs = (
        P(("groups", "rows"), "seq", None),
        P(("groups", "rows"), "seq", None),
        P("seq", None),
        P("seq", None),
        P(("groups", "rows")),
        P(("groups", "rows"), "seq"),
    )
    out_specs = P(("groups", "seq"), "rows")

    return jax.shard_map(body, mesh=mesh, in_specs=in_specs, out_specs=out_specs, check_vma=False)
```

```python
import functools

import jax
import jax.numpy as jnp
from jax import lax
from jax.experimental import pallas as pl
from jax.experimental.pallas import tpu as pltpu
from jax.sharding import PartitionSpec as P


LANES = 128
VMEM = pl.BlockSpec(memory_space=pltpu.VMEM)
HBM = pl.BlockSpec(memory_space=pltpu.HBM)
SMEM = pl.BlockSpec(memory_space=pltpu.SMEM)


ROUTES = {
    "tokens": ((3, 2, 0, 1), (2, 3, 1, 0), (1, 0, 3, 2)),
    "scores": ((1, 2, 3, 0), (2, 3, 0, 1), (3, 0, 1, 2)),
}


def routes(stage, n):
    if n == 4 and stage in ROUTES:
        return ROUTES[stage]
    if n & (n - 1) == 0:
        order = list(range(n - 1, 0, -1))
        if stage == "tokens":
            order = order[:1] + order[:0:-1]
        return [tuple(d ^ k for d in range(n)) for k in order]
    return [tuple((d + k) % n for d in range(n)) for k in range(1, n)]


def inverse(route):
    return tuple(route.index(d) for d in range(len(route)))


def entry(route, d):
    if all(t == a ^ route[0] for a, t in enumerate(route)):
        return d ^ route[0]
    at = route[0]
    for a, t in enumerate(route[1:], 1):
        at = jnp.where(d == a, t, at)
    return at


def exchange(arrays, axis, n, stage):
    got = []
    for i, route in enumerate(routes(stage, n)):
        got.append(lax.ppermute(arrays[i], axis, list(enumerate(route))))
    return got


def in_place(array):
    return pltpu.with_memory_space_constraint(array, pltpu.HBM)


def call(kernel, outs, in_specs, scratch=(), mib=16):
    return pl.pallas_call(
        kernel,
        out_shape=[jax.ShapeDtypeStruct(*o) for o in outs],
        in_specs=list(in_specs),
        out_specs=[VMEM] * len(outs),
        scratch_shapes=list(scratch),
        compiler_params=pltpu.CompilerParams(vmem_limit_bytes=mib << 20),
    )


def slice_copies(sources, at, width, out, sem):
    at = pl.multiple_of(at * width, width)
    return [
        pltpu.make_async_copy(src.at[0, :, pl.ds(at, width)], out.at[j], sem.at[j])
        for j, src in enumerate(sources)
    ]


def run_all(copies):
    for c in copies:
        c.start()
    for c in copies:
        c.wait()


def pack_kernel(x, g, *rest, n, width):
    outs, sem = rest[:-1], rest[-1]
    s = lax.axis_index("seq")
    copies = []
    for i, route in enumerate(routes("tokens", n)):
        copies += slice_copies((x, g), entry(route, s), width, outs[i], sem.at[i])
    run_all(copies)


def fetch_kernel(after, x, g, *rest, width):
    count = (len(rest) - 3) // 2
    sources, outs, own = rest[:count], rest[count : 2 * count], rest[2 * count]
    own_sem, sem = rest[2 * count + 1 :]
    copies = slice_copies((x, g), lax.axis_index("seq"), width, own, own_sem)
    for j, (src, out) in enumerate(zip(sources, outs)):
        copies.append(pltpu.make_async_copy(src, out, sem.at[j]))
    run_all(copies)


def feature_kernel(*refs, n, n_tok, block):
    toks, w_in, w_out = refs[:n], refs[n], refs[n + 1]
    outs, rows = refs[n + 2 : 2 * n + 2], refs[2 * n + 2]
    s = lax.axis_index("seq")
    source = [s] + [entry(inverse(route), s) for route in routes("tokens", n)]
    to = [s] + [entry(route, s) for route in routes("features", n)]
    total = n * n_tok
    for k in range(n):
        at = pl.multiple_of(source[k] * n_tok, n_tok)
        for j in range(2):
            rows[j, pl.ds(at, n_tok), :] = toks[k][j]
    first = jnp.dot(rows[0], w_in[...], preferred_element_type=jnp.float32)
    second = jnp.dot(rows[1], w_out[...], preferred_element_type=jnp.float32)
    turned = refs[2 * n + 3]
    for c in range(total // LANES):
        turned[c] = second[c * LANES : (c + 1) * LANES].T
    for k in range(n):
        at = pl.multiple_of(to[k] * block, block)
        outs[k][:total] = first
        for c in range(total // LANES):
            outs[k][total + c * block : total + (c + 1) * block] = turned[c, pl.ds(at, block), :]


def gradient_kernel(length, *refs, n, total, block):
    parts, out = refs[:n], refs[n]
    whole = parts[0][...]
    for part in parts[1:]:
        whole = whole + part[...]
    acc = None
    for c in range(total // LANES):
        feat_out = whole[total + c * block : total + (c + 1) * block]
        at = c * LANES + lax.broadcasted_iota(jnp.int32, feat_out.shape, 1)
        feat_out = jnp.where(at < length[0], feat_out, 0.0)
        prod = jnp.dot(
            feat_out,
            whole[c * LANES : (c + 1) * LANES],
            precision=lax.Precision.HIGHEST,
            preferred_element_type=jnp.float32,
        )
        acc = prod if acc is None else acc + prod
    out[...] = acc


def lane_scores(grads, store, block, step, sums):
    m = len(grads)

    def rows_step(t, carry):
        at = pl.multiple_of(t * step, step)
        acc = [jnp.zeros((step, LANES), jnp.float32) for _ in range(m)]
        for i in range(block):
            tile = store[pl.ds(at, step), i * LANES : (i + 1) * LANES]
            for k in range(m):
                acc[k] = acc[k] + tile * grads[k][i : i + 1, :]
        for k in range(m):
            sums[k, pl.ds(at, step), :] = acc[k]
        return carry

    lax.fori_loop(0, store.shape[0] // step, rows_step, 0)
    return [jnp.sum(sums[k].T, axis=0, keepdims=True) for k in range(m)]


def early_kernel(*refs, block, step):
    grads, (store, out, sums) = refs[:-3], refs[-3:]
    for k, row in enumerate(lane_scores(grads, store, block, step, sums)):
        out[k] = row


def late_kernel(early, *refs, n, m, first, late, block, step):
    grads, store = refs[: len(late)], refs[len(late)]
    outs, (rows, sums) = refs[len(late) + 1 : -2], refs[-2:]
    s, r = lax.axis_index("seq"), lax.axis_index("rows")
    query = [r] + [entry(inverse(route), r) for route in routes("gradient", m)]
    for j, k in enumerate(first):
        rows[query[k]] = early[j]
    for k, row in zip(late, lane_scores(grads, store, block, step, sums)):
        rows[query[k]] = row
    for k, target in enumerate([s] + [entry(route, s) for route in routes("scores", n)]):
        outs[k][...] = rows[target]


def body(layer_inputs, out_grads, input_proj, grad_proj, query_lengths, train_store):
    n, m = lax.axis_size("seq"), lax.axis_size("rows")
    _, n_tok, _ = layer_inputs.shape
    total = n * n_tok
    part, feats = input_proj.shape
    n_rows, coords = train_store.shape
    block = coords // feats
    f32 = jnp.float32

    tokens_in = in_place(layer_inputs), in_place(out_grads)
    slices = ((2, n_tok, part), layer_inputs.dtype)
    packed = call(
        functools.partial(pack_kernel, n=n, width=part),
        [slices] * (n - 1),
        [HBM, HBM],
        [pltpu.SemaphoreType.DMA((n - 1, 2))],
    )(*tokens_in)
    held = (input_proj, grad_proj, train_store)
    input_proj, grad_proj, train_store, own = call(
        functools.partial(fetch_kernel, width=part),
        [(a.shape, a.dtype) for a in held] + [slices],
        [VMEM] + [HBM] * 5,
        [pltpu.SemaphoreType.DMA((2,)), pltpu.SemaphoreType.DMA((3,))],
    )(packed[0], *tokens_in, *map(in_place, held))
    tokens = [own] + exchange(packed, "seq", n, "tokens")

    height = total + total * block // LANES
    partial = call(
        functools.partial(feature_kernel, n=n, n_tok=n_tok, block=block),
        [((height, LANES), f32)] * n,
        [VMEM] * (n + 2),
        [pltpu.VMEM((2, total, part), layer_inputs.dtype), pltpu.VMEM((total // LANES, feats, LANES), f32)],
    )(*tokens, input_proj, grad_proj)
    parts = [partial[0]] + exchange(partial[1:], "seq", n, "features")

    (grad,) = call(
        functools.partial(gradient_kernel, n=n, total=total, block=block),
        [((block, LANES), f32)],
        [SMEM] + [VMEM] * n,
    )(query_lengths, *parts)
    grads = [grad] + exchange([grad] * (m - 1), "rows", m, "gradient")

    first, late = (0, m - 1), tuple(range(1, m - 1))
    (early,) = call(
        functools.partial(early_kernel, block=block, step=128),
        [((len(first), 1, n_rows), f32)],
        [VMEM] * (len(first) + 1),
        [pltpu.VMEM((len(first), n_rows, LANES), f32)],
    )(*(grads[k] for k in first), train_store)
    step = 128 if len(late) <= 4 else 8
    scores = call(
        functools.partial(late_kernel, n=n, m=m, first=first, late=late, block=block, step=step),
        [((1, n_rows), f32)] * n,
        [VMEM] * (len(late) + 2),
        [pltpu.VMEM((m, 1, n_rows), f32), pltpu.VMEM((len(late), n_rows, LANES), f32)],
    )(early, *(grads[k] for k in late), train_store)
    out = scores[0]
    for other in exchange(scores[1:], "seq", n, "scores"):
        out = out + other
    return out


def solution(mesh):
    in_specs = (
        P(("groups", "rows"), "seq", None),
        P(("groups", "rows"), "seq", None),
        P("seq", None),
        P("seq", None),
        P(("groups", "rows")),
        P(("groups", "rows"), "seq"),
    )
    out_specs = P(("groups", "seq"), "rows")

    return jax.shard_map(body, mesh=mesh, in_specs=in_specs, out_specs=out_specs, check_vma=False)
```

```python
import functools

import jax
import jax.numpy as jnp
from jax import lax
from jax.experimental import pallas as pl
from jax.experimental.pallas import tpu as pltpu
from jax.sharding import PartitionSpec as P


LANES = 128
VMEM = pl.BlockSpec(memory_space=pltpu.VMEM)
HBM = pl.BlockSpec(memory_space=pltpu.HBM)
SMEM = pl.BlockSpec(memory_space=pltpu.SMEM)


ROUTES = {
    "features": ((2, 3, 0, 1), (1, 2, 3, 0), (3, 0, 1, 2)),
    "tokens": ((3, 2, 0, 1), (2, 3, 1, 0), (1, 0, 3, 2)),
    "scores": ((1, 2, 3, 0), (2, 3, 0, 1), (3, 0, 1, 2)),
}


def routes(stage, n):
    if n == 4 and stage in ROUTES:
        return ROUTES[stage]
    if n & (n - 1) == 0:
        order = list(range(n - 1, 0, -1))
        if stage == "tokens":
            order = order[:1] + order[:0:-1]
        return [tuple(d ^ k for d in range(n)) for k in order]
    return [tuple((d + k) % n for d in range(n)) for k in range(1, n)]


def inverse(route):
    return tuple(route.index(d) for d in range(len(route)))


def entry(route, d):
    if all(t == a ^ route[0] for a, t in enumerate(route)):
        return d ^ route[0]
    at = route[0]
    for a, t in enumerate(route[1:], 1):
        at = jnp.where(d == a, t, at)
    return at


def exchange(arrays, axis, n, stage):
    got = []
    for i, route in enumerate(routes(stage, n)):
        got.append(lax.ppermute(arrays[i], axis, list(enumerate(route))))
    return got


def in_place(array):
    return pltpu.with_memory_space_constraint(array, pltpu.HBM)


def call(kernel, outs, in_specs, scratch=(), mib=16):
    return pl.pallas_call(
        kernel,
        out_shape=[jax.ShapeDtypeStruct(*o) for o in outs],
        in_specs=list(in_specs),
        out_specs=[VMEM] * len(outs),
        scratch_shapes=list(scratch),
        compiler_params=pltpu.CompilerParams(vmem_limit_bytes=mib << 20),
    )


def slice_copies(sources, at, width, out, sem):
    at = pl.multiple_of(at * width, width)
    return [
        pltpu.make_async_copy(src.at[0, :, pl.ds(at, width)], out.at[j], sem.at[j])
        for j, src in enumerate(sources)
    ]


def run_all(copies):
    for c in copies:
        c.start()
    for c in copies:
        c.wait()


def pack_kernel(x, g, *rest, n, width):
    outs, sem = rest[:-1], rest[-1]
    s = lax.axis_index("seq")
    copies = []
    for i, route in enumerate(routes("tokens", n)):
        copies += slice_copies((x, g), entry(route, s), width, outs[i], sem.at[i])
    run_all(copies)


def fetch_kernel(after, x, g, *rest, width):
    count = (len(rest) - 3) // 2
    sources, outs, own = rest[:count], rest[count : 2 * count], rest[2 * count]
    own_sem, sem = rest[2 * count + 1 :]
    copies = slice_copies((x, g), lax.axis_index("seq"), width, own, own_sem)
    for j, (src, out) in enumerate(zip(sources, outs)):
        copies.append(pltpu.make_async_copy(src, out, sem.at[j]))
    run_all(copies)


def feature_kernel(*refs, n, n_tok, block):
    toks, w_in, w_out = refs[:n], refs[n], refs[n + 1]
    outs, rows = refs[n + 2 : 2 * n + 2], refs[2 * n + 2]
    s = lax.axis_index("seq")
    source = [s] + [entry(inverse(route), s) for route in routes("tokens", n)]
    to = [s] + [entry(route, s) for route in routes("features", n)]
    total = n * n_tok
    for k in range(n):
        at = pl.multiple_of(source[k] * n_tok, n_tok)
        for j in range(2):
            rows[j, pl.ds(at, n_tok), :] = toks[k][j]
    first = jnp.dot(rows[0], w_in[...], preferred_element_type=jnp.float32)
    second = jnp.dot(rows[1], w_out[...], preferred_element_type=jnp.float32)
    turned = refs[2 * n + 3]
    for c in range(total // LANES):
        turned[c] = second[c * LANES : (c + 1) * LANES].T
    for k in range(n):
        at = pl.multiple_of(to[k] * block, block)
        outs[k][:total] = first
        for c in range(total // LANES):
            outs[k][total + c * block : total + (c + 1) * block] = turned[c, pl.ds(at, block), :]


def gradient_kernel(length, *refs, n, total, block):
    parts, out = refs[:n], refs[n]
    whole = parts[0][...]
    for part in parts[1:]:
        whole = whole + part[...]
    acc = None
    for c in range(total // LANES):
        feat_out = whole[total + c * block : total + (c + 1) * block]
        at = c * LANES + lax.broadcasted_iota(jnp.int32, feat_out.shape, 1)
        feat_out = jnp.where(at < length[0], feat_out, 0.0)
        prod = jnp.dot(
            feat_out,
            whole[c * LANES : (c + 1) * LANES],
            precision=lax.Precision.HIGHEST,
            preferred_element_type=jnp.float32,
        )
        acc = prod if acc is None else acc + prod
    out[...] = acc


def lane_scores(grads, store, block, step, sums):
    m = len(grads)

    def rows_step(t, carry):
        at = pl.multiple_of(t * step, step)
        acc = [jnp.zeros((step, LANES), jnp.float32) for _ in range(m)]
        for i in range(block):
            tile = store[pl.ds(at, step), i * LANES : (i + 1) * LANES]
            for k in range(m):
                acc[k] = acc[k] + tile * grads[k][i : i + 1, :]
        for k in range(m):
            sums[k, pl.ds(at, step), :] = acc[k]
        return carry

    lax.fori_loop(0, store.shape[0] // step, rows_step, 0)
    return [jnp.sum(sums[k].T, axis=0, keepdims=True) for k in range(m)]


def step_for(group, n_rows):
    step = 256 // len(group) // 8 * 8
    while n_rows % step:
        step -= 8
    return step


def early_kernel(*refs, count, block, step):
    grads, (store, out, sums) = refs[:count], refs[-3:]
    for k, row in enumerate(lane_scores(grads, store, block, step, sums)):
        out[k] = row


def late_kernel(*refs, n, m, groups, block, step):
    ready, late = groups[:-1], groups[-1]
    done, refs = refs[: len(ready)], refs[len(ready) :]
    grads, store = refs[: len(late)], refs[len(late)]
    outs, (rows, sums) = refs[len(late) + 1 : -2], refs[-2:]
    s, r = lax.axis_index("seq"), lax.axis_index("rows")
    query = [r] + [entry(inverse(route), r) for route in routes("gradient", m)]
    for group, part in zip(ready, done):
        for j, k in enumerate(group):
            rows[query[k]] = part[j]
    for k, row in zip(late, lane_scores(grads, store, block, step, sums)):
        rows[query[k]] = row
    for k, target in enumerate([s] + [entry(route, s) for route in routes("scores", n)]):
        outs[k][...] = rows[target]


def body(layer_inputs, out_grads, input_proj, grad_proj, query_lengths, train_store):
    n, m = lax.axis_size("seq"), lax.axis_size("rows")
    _, n_tok, _ = layer_inputs.shape
    total = n * n_tok
    part, feats = input_proj.shape
    n_rows, coords = train_store.shape
    block = coords // feats
    f32 = jnp.float32

    tokens_in = in_place(layer_inputs), in_place(out_grads)
    slices = ((2, n_tok, part), layer_inputs.dtype)
    packed = call(
        functools.partial(pack_kernel, n=n, width=part),
        [slices] * (n - 1),
        [HBM, HBM],
        [pltpu.SemaphoreType.DMA((n - 1, 2))],
    )(*tokens_in)
    held = (input_proj, grad_proj, train_store)
    input_proj, grad_proj, train_store, own = call(
        functools.partial(fetch_kernel, width=part),
        [(a.shape, a.dtype) for a in held] + [slices],
        [VMEM] + [HBM] * 5,
        [pltpu.SemaphoreType.DMA((2,)), pltpu.SemaphoreType.DMA((3,))],
    )(packed[0], *tokens_in, *map(in_place, held))
    tokens = [own] + exchange(packed, "seq", n, "tokens")

    height = total + total * block // LANES
    partial = call(
        functools.partial(feature_kernel, n=n, n_tok=n_tok, block=block),
        [((height, LANES), f32)] * n,
        [VMEM] * (n + 2),
        [pltpu.VMEM((2, total, part), layer_inputs.dtype), pltpu.VMEM((total // LANES, feats, LANES), f32)],
    )(*tokens, input_proj, grad_proj)
    parts = [partial[0]] + exchange(partial[1:], "seq", n, "features")

    (grad,) = call(
        functools.partial(gradient_kernel, n=n, total=total, block=block),
        [((block, LANES), f32)],
        [SMEM] + [VMEM] * n,
    )(query_lengths, *parts)
    grads = [grad] + exchange([grad] * (m - 1), "rows", m, "gradient")

    groups = ((0, m - 1), tuple(range(1, m // 2)), tuple(range(m // 2, m - 1)))
    ready = []
    for group in groups[:-1]:
        ready += call(
            functools.partial(early_kernel, count=len(group), block=block, step=step_for(group, n_rows)),
            [((len(group), 1, n_rows), f32)],
            [VMEM] * (len(group) + 1 + len(ready)),
            [pltpu.VMEM((len(group), n_rows, LANES), f32)],
        )(*(grads[k] for k in group), *ready, train_store)
    late = groups[-1]
    step = step_for(late, n_rows)
    scores = call(
        functools.partial(late_kernel, n=n, m=m, groups=groups, block=block, step=step),
        [((1, n_rows), f32)] * n,
        [VMEM] * (len(ready) + len(late) + 1),
        [pltpu.VMEM((m, 1, n_rows), f32), pltpu.VMEM((len(late), n_rows, LANES), f32)],
    )(*ready, *(grads[k] for k in late), train_store)
    out = scores[0]
    for other in exchange(scores[1:], "seq", n, "scores"):
        out = out + other
    return out


def solution(mesh):
    in_specs = (
        P(("groups", "rows"), "seq", None),
        P(("groups", "rows"), "seq", None),
        P("seq", None),
        P("seq", None),
        P(("groups", "rows")),
        P(("groups", "rows"), "seq"),
    )
    out_specs = P(("groups", "seq"), "rows")

    return jax.shard_map(body, mesh=mesh, in_specs=in_specs, out_specs=out_specs, check_vma=False)
```

```python
import functools

import jax
import jax.numpy as jnp
from jax import lax
from jax.experimental import pallas as pl
from jax.experimental.pallas import tpu as pltpu
from jax.sharding import PartitionSpec as P


LANES = 128
VMEM = pl.BlockSpec(memory_space=pltpu.VMEM)
HBM = pl.BlockSpec(memory_space=pltpu.HBM)
SMEM = pl.BlockSpec(memory_space=pltpu.SMEM)


ROUTES = {
    "features": ((2, 3, 0, 1), (1, 2, 3, 0), (3, 0, 1, 2)),
    "tokens": ((3, 2, 0, 1), (2, 3, 1, 0), (1, 0, 3, 2)),
    "scores": ((1, 2, 3, 0), (2, 3, 0, 1), (3, 0, 1, 2)),
}


def routes(stage, n):
    if n == 4 and stage in ROUTES:
        return ROUTES[stage]
    if n & (n - 1) == 0:
        order = list(range(n - 1, 0, -1))
        if stage == "tokens":
            order = order[:1] + order[:0:-1]
        return [tuple(d ^ k for d in range(n)) for k in order]
    return [tuple((d + k) % n for d in range(n)) for k in range(1, n)]


def inverse(route):
    return tuple(route.index(d) for d in range(len(route)))


def entry(route, d):
    if all(t == a ^ route[0] for a, t in enumerate(route)):
        return d ^ route[0]
    at = route[0]
    for a, t in enumerate(route[1:], 1):
        at = jnp.where(d == a, t, at)
    return at


def exchange(arrays, axis, n, stage):
    got = []
    for i, route in enumerate(routes(stage, n)):
        got.append(lax.ppermute(arrays[i], axis, list(enumerate(route))))
    return got


def in_place(array):
    return pltpu.with_memory_space_constraint(array, pltpu.HBM)


def call(kernel, outs, in_specs, scratch=(), mib=16):
    return pl.pallas_call(
        kernel,
        out_shape=[jax.ShapeDtypeStruct(*o) for o in outs],
        in_specs=list(in_specs),
        out_specs=[VMEM] * len(outs),
        scratch_shapes=list(scratch),
        compiler_params=pltpu.CompilerParams(vmem_limit_bytes=mib << 20),
    )


def slice_copies(sources, at, width, out, sem):
    at = pl.multiple_of(at * width, width)
    return [
        pltpu.make_async_copy(src.at[0, :, pl.ds(at, width)], out.at[j], sem.at[j])
        for j, src in enumerate(sources)
    ]


def run_all(copies):
    for c in copies:
        c.start()
    for c in copies:
        c.wait()


def pack_kernel(x, g, *rest, n, width):
    outs, sem = rest[:-1], rest[-1]
    s = lax.axis_index("seq")
    copies = []
    for i, route in enumerate(routes("tokens", n)):
        copies += slice_copies((x, g), entry(route, s), width, outs[i], sem.at[i])
    run_all(copies)


def fetch_kernel(after, x, g, *rest, width):
    count = (len(rest) - 3) // 2
    sources, outs, own = rest[:count], rest[count : 2 * count], rest[2 * count]
    own_sem, sem = rest[2 * count + 1 :]
    copies = slice_copies((x, g), lax.axis_index("seq"), width, own, own_sem)
    for j, (src, out) in enumerate(zip(sources, outs)):
        copies.append(pltpu.make_async_copy(src, out, sem.at[j]))
    run_all(copies)


def feature_kernel(*refs, n, n_tok, block):
    toks, w_in, w_out = refs[:n], refs[n], refs[n + 1]
    outs, rows = refs[n + 2 : 2 * n + 2], refs[2 * n + 2]
    s = lax.axis_index("seq")
    source = [s] + [entry(inverse(route), s) for route in routes("tokens", n)]
    to = [s] + [entry(route, s) for route in routes("features", n)]
    total = n * n_tok
    for k in range(n):
        at = pl.multiple_of(source[k] * n_tok, n_tok)
        for j in range(2):
            rows[j, pl.ds(at, n_tok), :] = toks[k][j]
    first = jnp.dot(rows[0], w_in[...], preferred_element_type=jnp.float32)
    outT = lax.dot_general(
        w_out[...], rows[1], (((0,), (1,)), ((), ())), preferred_element_type=jnp.float32
    )
    turned = refs[2 * n + 3]
    for c in range(total // LANES):
        turned[c] = outT[:, c * LANES : (c + 1) * LANES]
    for k in range(n):
        at = pl.multiple_of(to[k] * block, block)
        outs[k][:total] = first
        for c in range(total // LANES):
            outs[k][total + c * block : total + (c + 1) * block] = turned[c, pl.ds(at, block), :]


def gradient_kernel(length, *refs, n, total, block):
    parts, out = refs[:n], refs[n]
    whole = parts[0][...]
    for part in parts[1:]:
        whole = whole + part[...]
    acc = None
    for c in range(total // LANES):
        feat_out = whole[total + c * block : total + (c + 1) * block]
        at = c * LANES + lax.broadcasted_iota(jnp.int32, feat_out.shape, 1)
        feat_out = jnp.where(at < length[0], feat_out, 0.0)
        prod = jnp.dot(
            feat_out,
            whole[c * LANES : (c + 1) * LANES],
            precision=lax.Precision.HIGHEST,
            preferred_element_type=jnp.float32,
        )
        acc = prod if acc is None else acc + prod
    out[...] = acc


def lane_scores(grads, store, block, step, sums):
    m = len(grads)

    def rows_step(t, carry):
        at = pl.multiple_of(t * step, step)
        acc = [jnp.zeros((step, LANES), jnp.float32) for _ in range(m)]
        for i in range(block):
            tile = store[pl.ds(at, step), i * LANES : (i + 1) * LANES]
            for k in range(m):
                acc[k] = acc[k] + tile * grads[k][i : i + 1, :]
        for k in range(m):
            sums[k, pl.ds(at, step), :] = acc[k]
        return carry

    lax.fori_loop(0, store.shape[0] // step, rows_step, 0)
    return [jnp.sum(sums[k].T, axis=0, keepdims=True) for k in range(m)]


def step_for(group, n_rows):
    step = 256 // len(group) // 8 * 8
    while n_rows % step:
        step -= 8
    return step


def early_kernel(*refs, count, block, step):
    grads, (store, out, sums) = refs[:count], refs[-3:]
    for k, row in enumerate(lane_scores(grads, store, block, step, sums)):
        out[k] = row


def late_kernel(*refs, n, m, groups, block, step):
    ready, late = groups[:-1], groups[-1]
    done, refs = refs[: len(ready)], refs[len(ready) :]
    grads, store = refs[: len(late)], refs[len(late)]
    outs, (rows, sums) = refs[len(late) + 1 : -2], refs[-2:]
    s, r = lax.axis_index("seq"), lax.axis_index("rows")
    query = [r] + [entry(inverse(route), r) for route in routes("gradient", m)]
    for group, part in zip(ready, done):
        for j, k in enumerate(group):
            rows[query[k]] = part[j]
    for k, row in zip(late, lane_scores(grads, store, block, step, sums)):
        rows[query[k]] = row
    for k, target in enumerate([s] + [entry(route, s) for route in routes("scores", n)]):
        outs[k][...] = rows[target]


def body(layer_inputs, out_grads, input_proj, grad_proj, query_lengths, train_store):
    n, m = lax.axis_size("seq"), lax.axis_size("rows")
    _, n_tok, _ = layer_inputs.shape
    total = n * n_tok
    part, feats = input_proj.shape
    n_rows, coords = train_store.shape
    block = coords // feats
    f32 = jnp.float32

    tokens_in = in_place(layer_inputs), in_place(out_grads)
    slices = ((2, n_tok, part), layer_inputs.dtype)
    packed = call(
        functools.partial(pack_kernel, n=n, width=part),
        [slices] * (n - 1),
        [HBM, HBM],
        [pltpu.SemaphoreType.DMA((n - 1, 2))],
    )(*tokens_in)
    held = (input_proj, grad_proj, train_store)
    input_proj, grad_proj, train_store, own = call(
        functools.partial(fetch_kernel, width=part),
        [(a.shape, a.dtype) for a in held] + [slices],
        [VMEM] + [HBM] * 5,
        [pltpu.SemaphoreType.DMA((2,)), pltpu.SemaphoreType.DMA((3,))],
    )(packed[0], *tokens_in, *map(in_place, held))
    tokens = [own] + exchange(packed, "seq", n, "tokens")

    height = total + total * block // LANES
    partial = call(
        functools.partial(feature_kernel, n=n, n_tok=n_tok, block=block),
        [((height, LANES), f32)] * n,
        [VMEM] * (n + 2),
        [pltpu.VMEM((2, total, part), layer_inputs.dtype), pltpu.VMEM((total // LANES, feats, LANES), f32)],
    )(*tokens, input_proj, grad_proj)
    parts = [partial[0]] + exchange(partial[1:], "seq", n, "features")

    (grad,) = call(
        functools.partial(gradient_kernel, n=n, total=total, block=block),
        [((block, LANES), f32)],
        [SMEM] + [VMEM] * n,
    )(query_lengths, *parts)
    grads = [grad] + exchange([grad] * (m - 1), "rows", m, "gradient")

    groups = ((0,), (m - 1,), tuple(range(1, m // 2)), tuple(range(m // 2, m - 1)))
    ready = []
    for group in groups[:-1]:
        ready += call(
            functools.partial(early_kernel, count=len(group), block=block, step=step_for(group, n_rows)),
            [((len(group), 1, n_rows), f32)],
            [VMEM] * (len(group) + 1 + len(ready)),
            [pltpu.VMEM((len(group), n_rows, LANES), f32)],
        )(*(grads[k] for k in group), *ready, train_store)
    late = groups[-1]
    step = step_for(late, n_rows)
    scores = call(
        functools.partial(late_kernel, n=n, m=m, groups=groups, block=block, step=step),
        [((1, n_rows), f32)] * n,
        [VMEM] * (len(ready) + len(late) + 1),
        [pltpu.VMEM((m, 1, n_rows), f32), pltpu.VMEM((len(late), n_rows, LANES), f32)],
    )(*ready, *(grads[k] for k in late), train_store)
    out = scores[0]
    for other in exchange(scores[1:], "seq", n, "scores"):
        out = out + other
    return out


def solution(mesh):
    in_specs = (
        P(("groups", "rows"), "seq", None),
        P(("groups", "rows"), "seq", None),
        P("seq", None),
        P("seq", None),
        P(("groups", "rows")),
        P(("groups", "rows"), "seq"),
    )
    out_specs = P(("groups", "seq"), "rows")

    return jax.shard_map(body, mesh=mesh, in_specs=in_specs, out_specs=out_specs, check_vma=False)
```

```python
import functools

import jax
import jax.numpy as jnp
from jax import lax
from jax.experimental import pallas as pl
from jax.experimental.pallas import tpu as pltpu
from jax.sharding import PartitionSpec as P


LANES = 128
VMEM = pl.BlockSpec(memory_space=pltpu.VMEM)
HBM = pl.BlockSpec(memory_space=pltpu.HBM)
SMEM = pl.BlockSpec(memory_space=pltpu.SMEM)


ROUTES = {
    "features": ((2, 3, 0, 1), (1, 2, 3, 0), (3, 0, 1, 2)),
    "tokens": ((3, 2, 0, 1), (2, 3, 1, 0), (1, 0, 3, 2)),
    "scores": ((1, 2, 3, 0), (2, 3, 0, 1), (3, 0, 1, 2)),
}


def routes(stage, n):
    if n == 4 and stage in ROUTES:
        return ROUTES[stage]
    if n & (n - 1) == 0:
        order = list(range(n - 1, 0, -1))
        if stage == "tokens":
            order = order[:1] + order[:0:-1]
        return [tuple(d ^ k for d in range(n)) for k in order]
    return [tuple((d + k) % n for d in range(n)) for k in range(1, n)]


def inverse(route):
    return tuple(route.index(d) for d in range(len(route)))


def entry(route, d):
    if all(t == a ^ route[0] for a, t in enumerate(route)):
        return d ^ route[0]
    at = route[0]
    for a, t in enumerate(route[1:], 1):
        at = jnp.where(d == a, t, at)
    return at


def exchange(arrays, axis, n, stage):
    got = []
    for i, route in enumerate(routes(stage, n)):
        got.append(lax.ppermute(arrays[i], axis, list(enumerate(route))))
    return got


def in_place(array):
    return pltpu.with_memory_space_constraint(array, pltpu.HBM)


def call(kernel, outs, in_specs, scratch=(), mib=16):
    return pl.pallas_call(
        kernel,
        out_shape=[jax.ShapeDtypeStruct(*o) for o in outs],
        in_specs=list(in_specs),
        out_specs=[VMEM] * len(outs),
        scratch_shapes=list(scratch),
        compiler_params=pltpu.CompilerParams(vmem_limit_bytes=mib << 20),
    )


def slice_copies(sources, at, width, out, sem):
    at = pl.multiple_of(at * width, width)
    return [
        pltpu.make_async_copy(src.at[0, :, pl.ds(at, width)], out.at[j], sem.at[j])
        for j, src in enumerate(sources)
    ]


def run_all(copies):
    for c in copies:
        c.start()
    for c in copies:
        c.wait()


def pack_kernel(x, g, *rest, n, width):
    outs, sem = rest[:-1], rest[-1]
    s = lax.axis_index("seq")
    copies = []
    for i, route in enumerate(routes("tokens", n)):
        copies += slice_copies((x, g), entry(route, s), width, outs[i], sem.at[i])
    run_all(copies)


def fetch_kernel(after, x, g, *rest, width):
    count = (len(rest) - 4) // 2
    sources, outs, own = rest[:count], rest[count : 2 * count], rest[2 * count]
    own_sem, sem, straight = rest[2 * count + 1 :]
    copies = slice_copies((x, g), lax.axis_index("seq"), width, own, own_sem)
    for j, (src, out) in enumerate(zip(sources, outs)):
        copies.append(pltpu.make_async_copy(src, out if j != 1 else straight, sem.at[j]))
    run_all(copies)
    outs[1][...] = straight[...].T


def feature_kernel(*refs, n, n_tok, block):
    toks, w_in, w_out = refs[:n], refs[n], refs[n + 1]
    outs, rows = refs[n + 2 : 2 * n + 2], refs[2 * n + 2]
    s = lax.axis_index("seq")
    source = [s] + [entry(inverse(route), s) for route in routes("tokens", n)]
    to = [s] + [entry(route, s) for route in routes("features", n)]
    total = n * n_tok
    for k in range(n):
        at = pl.multiple_of(source[k] * n_tok, n_tok)
        for j in range(2):
            rows[j, pl.ds(at, n_tok), :] = toks[k][j]
    first = jnp.dot(rows[0], w_in[...], preferred_element_type=jnp.float32)
    outT = lax.dot_general(
        w_out[...], rows[1], (((1,), (1,)), ((), ())), preferred_element_type=jnp.float32
    )
    turned = refs[2 * n + 3]
    for c in range(total // LANES):
        turned[c] = outT[:, c * LANES : (c + 1) * LANES]
    for k in range(n):
        at = pl.multiple_of(to[k] * block, block)
        outs[k][:total] = first
        for c in range(total // LANES):
            outs[k][total + c * block : total + (c + 1) * block] = turned[c, pl.ds(at, block), :]


def gradient_kernel(length, *refs, n, total, block):
    parts, out = refs[:n], refs[n]
    whole = parts[0][...]
    for part in parts[1:]:
        whole = whole + part[...]
    acc = None
    for c in range(total // LANES):
        feat_out = whole[total + c * block : total + (c + 1) * block]
        at = c * LANES + lax.broadcasted_iota(jnp.int32, feat_out.shape, 1)
        feat_out = jnp.where(at < length[0], feat_out, 0.0)
        prod = jnp.dot(
            feat_out,
            whole[c * LANES : (c + 1) * LANES],
            precision=lax.Precision.HIGHEST,
            preferred_element_type=jnp.float32,
        )
        acc = prod if acc is None else acc + prod
    out[...] = acc


def lane_scores(grads, store, block, step, sums):
    m = len(grads)

    def rows_step(t, carry):
        at = pl.multiple_of(t * step, step)
        acc = [jnp.zeros((step, LANES), jnp.float32) for _ in range(m)]
        for i in range(block):
            tile = store[pl.ds(at, step), i * LANES : (i + 1) * LANES]
            for k in range(m):
                acc[k] = acc[k] + tile * grads[k][i : i + 1, :]
        for k in range(m):
            sums[k, pl.ds(at, step), :] = acc[k]
        return carry

    lax.fori_loop(0, store.shape[0] // step, rows_step, 0)
    return [jnp.sum(sums[k].T, axis=0, keepdims=True) for k in range(m)]


def step_for(group, n_rows):
    step = 256 // len(group) // 8 * 8
    while n_rows % step:
        step -= 8
    return step


def early_kernel(*refs, count, block, step):
    grads, (store, out, sums) = refs[:count], refs[-3:]
    for k, row in enumerate(lane_scores(grads, store, block, step, sums)):
        out[k] = row


def late_kernel(*refs, n, m, groups, block, step):
    ready, late = groups[:-1], groups[-1]
    done, refs = refs[: len(ready)], refs[len(ready) :]
    grads, store = refs[: len(late)], refs[len(late)]
    outs, (rows, sums) = refs[len(late) + 1 : -2], refs[-2:]
    s, r = lax.axis_index("seq"), lax.axis_index("rows")
    query = [r] + [entry(inverse(route), r) for route in routes("gradient", m)]
    for group, part in zip(ready, done):
        for j, k in enumerate(group):
            rows[query[k]] = part[j]
    for k, row in zip(late, lane_scores(grads, store, block, step, sums)):
        rows[query[k]] = row
    for k, target in enumerate([s] + [entry(route, s) for route in routes("scores", n)]):
        outs[k][...] = rows[target]


def body(layer_inputs, out_grads, input_proj, grad_proj, query_lengths, train_store):
    n, m = lax.axis_size("seq"), lax.axis_size("rows")
    _, n_tok, _ = layer_inputs.shape
    total = n * n_tok
    part, feats = input_proj.shape
    n_rows, coords = train_store.shape
    block = coords // feats
    f32 = jnp.float32

    tokens_in = in_place(layer_inputs), in_place(out_grads)
    slices = ((2, n_tok, part), layer_inputs.dtype)
    packed = call(
        functools.partial(pack_kernel, n=n, width=part),
        [slices] * (n - 1),
        [HBM, HBM],
        [pltpu.SemaphoreType.DMA((n - 1, 2))],
    )(*tokens_in)
    held = (input_proj, grad_proj, train_store)
    input_proj, grad_proj, train_store, own = call(
        functools.partial(fetch_kernel, width=part),
        [(a.shape if a is not grad_proj else a.shape[::-1], a.dtype) for a in held] + [slices],
        [VMEM] + [HBM] * 5,
        [pltpu.SemaphoreType.DMA((2,)), pltpu.SemaphoreType.DMA((3,)), pltpu.VMEM(grad_proj.shape, grad_proj.dtype)],
    )(packed[0], *tokens_in, *map(in_place, held))
    tokens = [own] + exchange(packed, "seq", n, "tokens")

    height = total + total * block // LANES
    partial = call(
        functools.partial(feature_kernel, n=n, n_tok=n_tok, block=block),
        [((height, LANES), f32)] * n,
        [VMEM] * (n + 2),
        [pltpu.VMEM((2, total, part), layer_inputs.dtype), pltpu.VMEM((total // LANES, feats, LANES), f32)],
    )(*tokens, input_proj, grad_proj)
    parts = [partial[0]] + exchange(partial[1:], "seq", n, "features")

    (grad,) = call(
        functools.partial(gradient_kernel, n=n, total=total, block=block),
        [((block, LANES), f32)],
        [SMEM] + [VMEM] * n,
    )(query_lengths, *parts)
    grads = [grad] + exchange([grad] * (m - 1), "rows", m, "gradient")

    groups = ((0,), (m - 1,), tuple(range(1, m // 2)), tuple(range(m // 2, m - 1)))
    ready = []
    for group in groups[:-1]:
        ready += call(
            functools.partial(early_kernel, count=len(group), block=block, step=step_for(group, n_rows)),
            [((len(group), 1, n_rows), f32)],
            [VMEM] * (len(group) + 1 + len(ready)),
            [pltpu.VMEM((len(group), n_rows, LANES), f32)],
        )(*(grads[k] for k in group), *ready, train_store)
    late = groups[-1]
    step = step_for(late, n_rows)
    scores = call(
        functools.partial(late_kernel, n=n, m=m, groups=groups, block=block, step=step),
        [((1, n_rows), f32)] * n,
        [VMEM] * (len(ready) + len(late) + 1),
        [pltpu.VMEM((m, 1, n_rows), f32), pltpu.VMEM((len(late), n_rows, LANES), f32)],
    )(*ready, *(grads[k] for k in late), train_store)
    out = scores[0]
    for other in exchange(scores[1:], "seq", n, "scores"):
        out = out + other
    return out


def solution(mesh):
    in_specs = (
        P(("groups", "rows"), "seq", None),
        P(("groups", "rows"), "seq", None),
        P("seq", None),
        P("seq", None),
        P(("groups", "rows")),
        P(("groups", "rows"), "seq"),
    )
    out_specs = P(("groups", "seq"), "rows")

    return jax.shard_map(body, mesh=mesh, in_specs=in_specs, out_specs=out_specs, check_vma=False)
```
